32 devices in a mesh: dom: 16 (over z, x, core), cell: 2 (over y).
Axes of the slice: x: 2, y: 2, z: 4, core: 2. Of those that a mesh axis runs over, the one named last changes fastest.
Arguments:
- models: bfloat16 [2, 512, 4096], P(None, 'dom', 'cell'), may hold values from -12 to 12
- gradients: bfloat16 [2, 512, 4096], P(None, 'dom', 'cell'), may hold values from -48 to 48
- length_scale: float32 [1], replicated, may hold values from 3 to 12
Outputs:
- update: float32 [2, 512, 4096], P(None, 'dom', 'cell')
The draws below stay inside these ranges and needn't reach their ends.
All inputs are finite; a program needn't handle non-finite values.
Results may differ from the reference program's by a relative error of at most 0.00045.
The reference program's roundings to bfloat16 on the way (of `kernel`) count: a program that leaves them out, or rounds other values in their place, can miss the bound.
Values may be sent and summed in bfloat16 or wider, within the bound.
A program may use at most 64 MiB of HBM per device.

```python
import math
import jax
import jax.numpy as jnp

P_SIZE = 512
NC = 4096


def draw_models(key, part):
    first, second, third = jax.random.split(key, 3)
    latent = jax.random.normal(first, (P_SIZE, 8), jnp.float32)
    basis_fields = jax.random.normal(second, (2, 8, NC), jnp.float32)
    jitter = 0.7 * jax.random.normal(third, (2, P_SIZE, NC), jnp.float32)
    fields = jnp.einsum('pk,jkc->jpc', latent, basis_fields) / math.sqrt(8.0) + jitter
    return jnp.clip(fields, -12.0, 12.0).astype(jnp.bfloat16)


def block_levels(stream_key, shape, pieces, smallest, largest):
    level = 1.0
    for position, shards_of in pieces:
        draws = jax.random.uniform(jax.random.fold_in(jax.random.fold_in(stream_key, 6), position), (shards_of,), jnp.float32, smallest / len(pieces), largest / len(pieces))
        level = level * jnp.repeat(jnp.exp(draws), shape[position] // shards_of).reshape((-1,) + (1,) * (len(shape) - 1 - position))
    return level


def scatter_about(rng, extent, spread, reach, pieces=(), kind=jnp.bfloat16):
    values = jax.random.normal(rng, extent, jnp.float32) * spread
    if len(pieces) > 0:
        values = block_levels(rng, extent, pieces, -0.22, 0.18) * values
    return jnp.clip(values, min=-reach, max=reach).astype(kind)


def setup_inputs(seed: int = 0) -> dict:
    key_of = jax.random.split(jax.random.key(seed), 4)
    return {
        "models": draw_models(jax.random.fold_in(key_of[3], 71), 0),
        "gradients": scatter_about(key_of[1], (2, P_SIZE, NC), 8.0, 48.0, ((1, 16), (2, 2))),
        "length_scale": jnp.clip(jnp.exp(jax.random.uniform(key_of[2], (1,), jnp.float32, math.log(3.0), math.log(12.0))), 3.0, 12.0),
    }


def reference(models, gradients, length_scale):
    scale_value = length_scale[0]
    wide_models = models.astype(jnp.float32)
    gram_sum = jnp.einsum("kpc,kqc->pq", wide_models, wide_models)
    squares = jnp.diagonal(gram_sum)
    distance = squares[:, None] + squares[None, :] - 2.0 * gram_sum
    kernel = jnp.exp(-distance / (scale_value * NC)).astype(jnp.bfloat16)
    wide_kernel = kernel.astype(jnp.float32)
    rowsum = jnp.sum(wide_kernel, axis=1)
    attract = jnp.einsum("pq,kqc->kpc", wide_kernel, gradients.astype(jnp.float32))
    pulled = jnp.einsum("pq,kqc->kpc", wide_kernel, wide_models)
    update = (attract + (2.0 / scale_value) * (rowsum[None, :, None] * wide_models - pulled)) / P_SIZE
    return update
```

```python
import functools
import math

import jax
import jax.numpy as jnp
from jax import lax
from jax.experimental import pallas as pl
from jax.experimental.pallas import tpu as pltpu
from jax.sharding import PartitionSpec as P

MESH = pl.DeviceIdType.MESH


def plain_body(models, gradients, length_scale):
    local_models, local_grads = (
        lax.all_to_all(models, "dom", split_axis=2, concat_axis=1, tiled=True),
        lax.all_to_all(gradients, "dom", split_axis=2, concat_axis=1, tiled=True),
    )
    cell_block = local_models.shape[2]
    particles = local_models.shape[1]
    cell_count = cell_block * lax.axis_size("dom") * lax.axis_size("cell")
    scale_value = length_scale[0]
    divisor = scale_value * cell_count
    partial_value = jnp.einsum(
        "kpc,kqc->pq", local_models, local_models, preferred_element_type=jnp.float32
    )
    summed = lax.psum(partial_value, "cell")
    row_block = lax.psum_scatter(summed, "dom", scatter_dimension=0, tiled=True)
    row_count = row_block.shape[0]
    row_start = lax.axis_index("dom") * row_count
    own_squares = jnp.diagonal(lax.dynamic_slice_in_dim(row_block, row_start, row_count, 1))
    squares = lax.all_gather(own_squares, "dom", axis=0, tiled=True)
    distance = own_squares[:, None] + squares[None, :] - 2.0 * row_block
    kernel = lax.all_gather(
        jnp.exp(-distance / divisor).astype(jnp.bfloat16), "dom", axis=0, tiled=True
    )
    rowsum = jnp.sum(kernel.astype(jnp.float32), axis=1)
    stacked = jnp.concatenate((local_grads, local_models), axis=2)
    product = jnp.einsum("pq,kqc->kpc", kernel, stacked, preferred_element_type=jnp.float32)
    attract = product[:, :, :cell_block]
    pulled = product[:, :, cell_block:]
    update = (
        attract
        + 2.0 / scale_value * (rowsum[None, :, None] * local_models.astype(jnp.float32) - pulled)
    ) / particles
    return lax.all_to_all(update, "dom", split_axis=1, concat_axis=2, tiled=True)


def stein_kernel(
    layers, group, planes,
    scale_ref, models_ref, grads_ref, out_ref,
    m_all, g_all, part, inbox, krows, base, outbox,
    local_sem, a2a_send, m_recv, g_recv, fwd_send,
    rs_send, rs_recv, k_send, k_recv, o_send, o_recv,
):
    fields, rows, width = models_ref.shape
    cells = width // group
    slab = group * rows
    count = layers * slab
    peers = group * planes
    piece = slab // peers
    total_cells = width * planes
    dom = lax.axis_index("dom")
    y = lax.axis_index("cell")
    z = dom // group
    g = dom % group
    me = g * planes + y
    has_up = z + 1 < layers
    has_down = z > 0

    def columns(which):
        return pl.ds(pl.multiple_of(which * cells, 128), cells)

    def layer_id(which):
        return (z * group + which // planes, which % planes)

    barrier = pltpu.get_barrier_semaphore()
    for k in range(1, peers):
        pl.semaphore_signal(
            barrier, inc=1, device_id=layer_id((me + k) % peers), device_id_type=MESH
        )

    @pl.when(has_up)
    def _():
        pl.semaphore_signal(barrier, inc=1, device_id=(dom + group, y), device_id_type=MESH)

    @pl.when(has_down)
    def _():
        pl.semaphore_signal(barrier, inc=1, device_id=(dom - group, y), device_id_type=MESH)

    tensors = ((models_ref, m_all, m_recv), (grads_ref, g_all, g_recv))
    locals_ = []
    for t, (src, dst, _) in enumerate(tensors):
        copy = pltpu.make_async_copy(
            src.at[:, :, columns(g)], dst.at[z, g], local_sem.at[t]
        )
        copy.start()
        locals_.append(copy)

    neighbours = jnp.where(has_up, 1, 0) + jnp.where(has_down, 1, 0)
    pl.semaphore_wait(barrier, peers - 1 + neighbours)

    pending = []
    for t, (src, dst, recv) in enumerate(tensors):
        for k in range(1, group):
            to = (g + k) % group
            copy = pltpu.make_async_remote_copy(
                src_ref=src.at[:, :, columns(to)],
                dst_ref=dst.at[z, g],
                send_sem=a2a_send.at[t, k],
                recv_sem=recv.at[z, g],
                device_id=(z * group + to, y),
                device_id_type=MESH,
            )
            copy.start()
            pending.append(copy)

    def hop(t, up, level, which, step, k):
        _, buf, recv = tensors[t]
        return pltpu.make_async_remote_copy(
            src_ref=buf.at[level, which],
            dst_ref=buf.at[level, which],
            send_sem=fwd_send.at[t, up, step, k],
            recv_sem=recv.at[level, which],
            device_id=(dom + group if up else dom - group, y),
            device_id_type=MESH,
        )

    def chain_step(t, step):
        for k in range(group):
            which = (g + group - k) % group
            if step == 0:
                if k == 0:
                    locals_[t].wait()
                else:
                    hop(t, 1, z, which, step, k).wait_recv()

                @pl.when(has_up)
                def _():
                    hop(t, 1, z, which, step, k).start()

                @pl.when(has_down)
                def _():
                    hop(t, 0, z, which, step, k).start()

                continue

            @pl.when(z >= step)
            def _():
                hop(t, 1, z - step, which, step, k).wait_recv()

                @pl.when(has_up)
                def _():
                    hop(t, 1, z - step, which, step, k).start()

            @pl.when(z + step < layers)
            def _():
                hop(t, 0, z + step, which, step, k).wait_recv()

                @pl.when(has_down)
                def _():
                    hop(t, 0, z + step, which, step, k).start()

    def chain_drain(t):
        for step in range(layers):
            for k in range(group):
                which = (g + group - k) % group

                @pl.when(jnp.logical_and(z >= step, has_up))
                def _():
                    hop(t, 1, z - step, which, step, k).wait_send()

                @pl.when(jnp.logical_and(z + step < layers, has_down))
                def _():
                    hop(t, 0, z + step, which, step, k).wait_send()

    def whole(buf, field):
        return buf[:, :, field].reshape(count, cells)

    for step in range(layers):
        chain_step(0, step)
    chain_step(1, 0)

    contract = (((1,), (1,)), ((), ()))
    gram = jnp.zeros((slab, count), jnp.float32)
    squares = jnp.zeros((8, count), jnp.float32)
    ones = jnp.ones((8, cells), jnp.bfloat16)
    for field in range(fields):
        every = whole(m_all, field)
        own = m_all[z, :, field].reshape(slab, cells)
        gram += lax.dot_general(own, every, contract, preferred_element_type=jnp.float32)
        wide = every.astype(jnp.float32)
        wide = wide * wide
        high = wide.astype(jnp.bfloat16)
        low = (wide - high.astype(jnp.float32)).astype(jnp.bfloat16)
        squares += lax.dot_general(ones, high, contract, preferred_element_type=jnp.float32)
        squares += lax.dot_general(ones, low, contract, preferred_element_type=jnp.float32)
    part[:, :piece, :] = gram.reshape(peers, piece, count)
    part[:, piece:, :] = jnp.broadcast_to(squares[None], (peers, 8, count))

    for k in range(1, peers):
        to = (me + k) % peers
        copy = pltpu.make_async_remote_copy(
            src_ref=part.at[to],
            dst_ref=inbox.at[me],
            send_sem=rs_send.at[k],
            recv_sem=rs_recv.at[me],
            device_id=layer_id(to),
            device_id_type=MESH,
        )
        copy.start()
        pending.append(copy)
    inbox[me] = part[me]

    if layers > 2:
        chain_step(1, 1)

    for k in range(1, peers):
        source = (me + peers - k) % peers
        pltpu.make_async_remote_copy(
            src_ref=part.at[source],
            dst_ref=inbox.at[source],
            send_sem=rs_send.at[k],
            recv_sem=rs_recv.at[source],
            device_id=layer_id(source),
            device_id_type=MESH,
        ).wait_recv()
    summed = inbox[0]
    for k in range(1, peers):
        summed = summed + inbox[k]
    row_gram = summed[:piece]
    row_squares = summed[piece:piece + 1]
    first = z * slab + me * piece
    row_index = lax.broadcasted_iota(jnp.int32, (piece, count), 0) + first
    col_index = lax.broadcasted_iota(jnp.int32, (piece, count), 1)
    own_squares = jnp.sum(
        jnp.where(row_index == col_index, row_gram, 0.0), axis=1, keepdims=True
    )
    scale = scale_ref[0]
    distance = own_squares + row_squares - 2.0 * row_gram
    divisor = jnp.full((piece, count), scale * total_cells, jnp.float32)
    krows[me] = jnp.exp(-distance / divisor).astype(jnp.bfloat16)

    for k in range(1, peers):
        to = (me + k) % peers
        copy = pltpu.make_async_remote_copy(
            src_ref=krows.at[me],
            dst_ref=krows.at[me],
            send_sem=k_send.at[k],
            recv_sem=k_recv.at[me],
            device_id=layer_id(to),
            device_id_type=MESH,
        )
        copy.start()
        pending.append(copy)
    for k in range(1, peers):
        source = (me + peers - k) % peers
        pltpu.make_async_remote_copy(
            src_ref=krows.at[source],
            dst_ref=krows.at[source],
            send_sem=k_send.at[k],
            recv_sem=k_recv.at[source],
            device_id=layer_id(source),
            device_id_type=MESH,
        ).wait_recv()

    kernel = krows[...].reshape(slab, count)
    rowsum = jnp.sum(kernel.astype(jnp.float32), axis=1, keepdims=True)
    factor = 2.0 / jnp.full((slab, cells), scale, jnp.float32)
    for field in range(fields):
        own = m_all[z, :, field].reshape(slab, cells).astype(jnp.float32)
        pulled = jnp.dot(kernel, whole(m_all, field), preferred_element_type=jnp.float32)
        base[field] = factor * (rowsum * own - pulled)

    for step in range(2 if layers > 2 else 1, layers):
        chain_step(1, step)

    def out_copy(field, to, source, k):
        return pltpu.make_async_remote_copy(
            src_ref=outbox.at[field, to],
            dst_ref=out_ref.at[field, :, columns(source)],
            send_sem=o_send.at[field, k],
            recv_sem=o_recv.at[field, source],
            device_id=(z * group + to, y),
            device_id_type=MESH,
        )

    for field in range(fields):
        attract = jnp.dot(kernel, whole(g_all, field), preferred_element_type=jnp.float32)
        update = (attract + base[field]) * (1.0 / count)
        outbox[field] = update.reshape(group, rows, cells)
        for k in range(1, group):
            copy = out_copy(field, (g + k) % group, g, k)
            copy.start()
            pending.append(copy)
        out_ref[field, :, columns(g)] = outbox[field, g]
    for field in range(fields):
        for k in range(1, group):
            source = (g + group - k) % group
            out_copy(field, source, source, k).wait_recv()
    chain_drain(0)
    chain_drain(1)
    for copy in pending:
        copy.wait_send()


def fused_body(layers, group, planes, models, gradients, length_scale):
    fields, rows, width = models.shape
    cells = width // group
    slab = group * rows
    count = layers * slab
    peers = group * planes
    piece = slab // peers
    dma = pltpu.SemaphoreType.DMA
    return pl.pallas_call(
        functools.partial(stein_kernel, layers, group, planes),
        out_shape=jax.ShapeDtypeStruct(models.shape, jnp.float32),
        in_specs=[
            pl.BlockSpec(memory_space=pltpu.SMEM),
            pl.BlockSpec(memory_space=pl.ANY),
            pl.BlockSpec(memory_space=pl.ANY),
        ],
        out_specs=pl.BlockSpec(memory_space=pltpu.VMEM),
        scratch_shapes=[
            pltpu.VMEM((layers, group, fields, rows, cells), jnp.bfloat16),
            pltpu.VMEM((layers, group, fields, rows, cells), jnp.bfloat16),
            pltpu.VMEM((peers, piece + 8, count), jnp.float32),
            pltpu.VMEM((peers, piece + 8, count), jnp.float32),
            pltpu.VMEM((peers, piece, count), jnp.bfloat16),
            pltpu.VMEM((fields, slab, cells), jnp.float32),
            pltpu.VMEM((fields, group, rows, cells), jnp.float32),
            dma((2,)),
            dma((2, group)),
            dma((layers, group)),
            dma((layers, group)),
            dma((2, 2, layers, group)),
            dma((peers,)),
            dma((peers,)),
            dma((peers,)),
            dma((peers,)),
            dma((fields, group)),
            dma((fields, group)),
        ],
        compiler_params=pltpu.CompilerParams(collective_id=0, has_side_effects=True),
        name="stein",
    )(length_scale, models, gradients)


def solution(mesh):
    spread, planes = mesh.shape["dom"], mesh.shape["cell"]
    layers = math.isqrt(spread)
    group = spread // layers

    def body(models, gradients, length_scale):
        _, rows, width = models.shape
        fits = (
            layers * group == spread
            and width % (group * 128) == 0
            and rows % 16 == 0
            and (group * rows) % (group * planes * 16) == 0
        )
        if not fits:
            return plain_body(models, gradients, length_scale)
        return fused_body(layers, group, planes, models, gradients, length_scale)

    placed = (P(None, "dom", "cell"), P(None, "dom", "cell"), P())
    return jax.shard_map(
        body, mesh=mesh, in_specs=placed, out_specs=P(None, "dom", "cell"), check_vma=False
    )
```

```python
import functools
import math

import jax
import jax.numpy as jnp
from jax import lax
from jax.experimental import pallas as pl
from jax.experimental.pallas import tpu as pltpu
from jax.sharding import PartitionSpec as P

MESH = pl.DeviceIdType.MESH


def plain_body(models, gradients, length_scale):
    local_models, local_grads = (
        lax.all_to_all(models, "dom", split_axis=2, concat_axis=1, tiled=True),
        lax.all_to_all(gradients, "dom", split_axis=2, concat_axis=1, tiled=True),
    )
    cell_block = local_models.shape[2]
    particles = local_models.shape[1]
    cell_count = cell_block * lax.axis_size("dom") * lax.axis_size("cell")
    scale_value = length_scale[0]
    divisor = scale_value * cell_count
    partial_value = jnp.einsum(
        "kpc,kqc->pq", local_models, local_models, preferred_element_type=jnp.float32
    )
    summed = lax.psum(partial_value, "cell")
    row_block = lax.psum_scatter(summed, "dom", scatter_dimension=0, tiled=True)
    row_count = row_block.shape[0]
    row_start = lax.axis_index("dom") * row_count
    own_squares = jnp.diagonal(lax.dynamic_slice_in_dim(row_block, row_start, row_count, 1))
    squares = lax.all_gather(own_squares, "dom", axis=0, tiled=True)
    distance = own_squares[:, None] + squares[None, :] - 2.0 * row_block
    kernel = lax.all_gather(
        jnp.exp(-distance / divisor).astype(jnp.bfloat16), "dom", axis=0, tiled=True
    )
    rowsum = jnp.sum(kernel.astype(jnp.float32), axis=1)
    stacked = jnp.concatenate((local_grads, local_models), axis=2)
    product = jnp.einsum("pq,kqc->kpc", kernel, stacked, preferred_element_type=jnp.float32)
    attract = product[:, :, :cell_block]
    pulled = product[:, :, cell_block:]
    update = (
        attract
        + 2.0 / scale_value * (rowsum[None, :, None] * local_models.astype(jnp.float32) - pulled)
    ) / particles
    return lax.all_to_all(update, "dom", split_axis=1, concat_axis=2, tiled=True)


def stein_kernel(
    layers, group, planes, held,
    scale_ref, models_ref, grads_ref, out_ref,
    m_all, g_all, part, inbox, swap_out, swap_in, krows, base, base_far, outbox, outbox_far,
    local_sem, a2a_send, m_recv, g_recv, fwd_send,
    rs_send, rs_recv, swap_sem, k_send, k_recv, o_send, o_recv,
):
    fields, rows, width = models_ref.shape
    cells = width // group
    slab = group * rows
    count = layers * slab
    peers = group * planes
    piece = slab // peers
    total_cells = width * planes
    spare = cells - held
    near = pl.ds(0, held)
    dom = lax.axis_index("dom")
    y = lax.axis_index("cell")
    z = dom // group
    g = dom % group
    me = g * planes + y
    has_up = z + 1 < layers
    has_down = z > 0
    is_end = jnp.logical_or(z == 0, z == layers - 1)
    is_inner = jnp.logical_and(z > 0, z < layers - 1)
    mate = z + 1 - 2 * (z % 2)
    up_end = z + 1 == layers - 1
    down_end = z - 1 == 0

    def both(left, right):
        return jnp.logical_and(left, right)

    def columns(which, start=0, size=None):
        return pl.ds(pl.multiple_of(which * cells + start, 128), cells if size is None else size)

    def layer_id(which):
        return (z * group + which // planes, which % planes)

    barrier = pltpu.get_barrier_semaphore()
    for k in range(1, peers):
        pl.semaphore_signal(
            barrier, inc=1, device_id=layer_id((me + k) % peers), device_id_type=MESH
        )
    for k in range(1, group):
        pl.semaphore_signal(
            barrier,
            inc=1,
            device_id=(mate * group + (g + k) % group, y),
            device_id_type=MESH,
        )

    @pl.when(has_up)
    def _():
        pl.semaphore_signal(barrier, inc=1, device_id=(dom + group, y), device_id_type=MESH)

    @pl.when(has_down)
    def _():
        pl.semaphore_signal(barrier, inc=1, device_id=(dom - group, y), device_id_type=MESH)

    tensors = ((models_ref, m_all, m_recv), (grads_ref, g_all, g_recv))
    locals_ = []
    for t, (src, dst, _) in enumerate(tensors):
        copy = pltpu.make_async_copy(
            src.at[:, :, columns(g)], dst.at[z, g], local_sem.at[t]
        )
        copy.start()
        locals_.append(copy)

    neighbours = jnp.where(has_up, 1, 0) + jnp.where(has_down, 1, 0)
    pl.semaphore_wait(barrier, peers - 1 + group - 1 + neighbours)

    pending = []
    for t, (src, dst, recv) in enumerate(tensors):
        for k in range(1, group):
            to = (g + k) % group
            copy = pltpu.make_async_remote_copy(
                src_ref=src.at[:, :, columns(to)],
                dst_ref=dst.at[z, g],
                send_sem=a2a_send.at[t, k],
                recv_sem=recv.at[z, g],
                device_id=(z * group + to, y),
                device_id_type=MESH,
            )
            copy.start()
            pending.append(copy)

    def hop(t, up, level, which, step, k, short):
        _, buf, recv = tensors[t]
        block = buf.at[level, which, :, :, near] if short else buf.at[level, which]
        return pltpu.make_async_remote_copy(
            src_ref=block,
            dst_ref=block,
            send_sem=fwd_send.at[t, up, step, k],
            recv_sem=recv.at[level, which],
            device_id=(dom + group if up else dom - group, y),
            device_id_type=MESH,
        )

    def push(t, up, level, which, step, k, verb):
        exists, short = (has_up, up_end) if up else (has_down, down_end)

        @pl.when(both(exists, short))
        def _():
            getattr(hop(t, up, level, which, step, k, True), verb)()

        @pl.when(both(exists, jnp.logical_not(short)))
        def _():
            getattr(hop(t, up, level, which, step, k, False), verb)()

    def chain_step(t, step):
        for k in range(group):
            which = (g + group - k) % group
            if step == 0:
                if k == 0:
                    locals_[t].wait()
                else:
                    hop(t, 1, z, which, step, k, False).wait_recv()
                push(t, 1, z, which, step, k, "start")
                push(t, 0, z, which, step, k, "start")
                continue

            @pl.when(z >= step)
            def _():
                @pl.when(is_end)
                def _():
                    hop(t, 1, z - step, which, step, k, True).wait_recv()

                @pl.when(is_inner)
                def _():
                    hop(t, 1, z - step, which, step, k, False).wait_recv()

                push(t, 1, z - step, which, step, k, "start")

            @pl.when(z + step < layers)
            def _():
                @pl.when(is_end)
                def _():
                    hop(t, 0, z + step, which, step, k, True).wait_recv()

                @pl.when(is_inner)
                def _():
                    hop(t, 0, z + step, which, step, k, False).wait_recv()

                push(t, 0, z + step, which, step, k, "start")

    def chain_drain(t):
        for step in range(layers):
            for k in range(group):
                which = (g + group - k) % group

                @pl.when(z >= step)
                def _():
                    push(t, 1, z - step, which, step, k, "wait_send")

                @pl.when(z + step < layers)
                def _():
                    push(t, 0, z + step, which, step, k, "wait_send")

    def every(buf, field, far):
        if far:
            return buf[:, :, field, :, held:].reshape(count, spare)
        return buf[:, :, field, :, :held].reshape(count, held)

    def one(level, field, far):
        if far:
            return m_all[level, :, field, :, held:].reshape(slab, spare)
        return m_all[level, :, field, :, :held].reshape(slab, held)

    contract = (((1,), (1,)), ((), ()))

    def inner_product(left, right):
        return lax.dot_general(left, right, contract, preferred_element_type=jnp.float32)

    for step in range(layers):
        chain_step(0, step)
    chain_step(1, 0)

    gram = jnp.zeros((slab, count), jnp.float32)
    for field in range(fields):
        gram += inner_product(one(z, field, False), every(m_all, field, False))
    part[:, :piece, :] = gram.reshape(peers, piece, count)

    @pl.when(is_inner)
    def _():
        own = jnp.zeros((slab, count), jnp.float32)
        other = jnp.zeros((slab, count), jnp.float32)
        squares = jnp.zeros((8, count), jnp.float32)
        for field in range(fields):
            far = every(m_all, field, True)
            own += inner_product(one(z, field, True), far)
            other += inner_product(one(mate, field, True), far)
            for block in (every(m_all, field, False), far):
                ones = jnp.ones((8, block.shape[1]), jnp.bfloat16)
                wide = block.astype(jnp.float32)
                wide = wide * wide
                high = wide.astype(jnp.bfloat16)
                low = (wide - high.astype(jnp.float32)).astype(jnp.bfloat16)
                squares += inner_product(ones, high)
                squares += inner_product(ones, low)
        part[:, :piece, :] += own.reshape(peers, piece, count)
        part[:, piece:2 * piece, :] = other.reshape(peers, piece, count)
        part[:, 2 * piece:, :] = jnp.broadcast_to(squares[None], (peers, 8, count))

    def rs_copy(to, slot, k, inner):
        span = pl.ds(0, 2 * piece + 8 if inner else piece)
        return pltpu.make_async_remote_copy(
            src_ref=part.at[to, span],
            dst_ref=inbox.at[slot, span],
            send_sem=rs_send.at[k],
            recv_sem=rs_recv.at[slot],
            device_id=layer_id(to),
            device_id_type=MESH,
        )

    def swap(inner):
        span = pl.ds(0, piece + 8 if inner else piece)
        return pltpu.make_async_remote_copy(
            src_ref=swap_out.at[span],
            dst_ref=swap_in.at[span],
            send_sem=swap_sem.at[0],
            recv_sem=swap_sem.at[1],
            device_id=(mate * group + g, y),
            device_id_type=MESH,
        )

    def k_copy(half, to, slot, k):
        return pltpu.make_async_remote_copy(
            src_ref=krows.at[half, slot],
            dst_ref=krows.at[half, slot],
            send_sem=k_send.at[half, k],
            recv_sem=k_recv.at[half, slot],
            device_id=layer_id(to),
            device_id_type=MESH,
        )

    scale = scale_ref[0]

    def make_rows(half, level, row_gram, row_squares):
        first = level * slab + me * piece
        row_index = lax.broadcasted_iota(jnp.int32, (piece, count), 0) + first
        col_index = lax.broadcasted_iota(jnp.int32, (piece, count), 1)
        own_squares = jnp.sum(
            jnp.where(row_index == col_index, row_gram, 0.0), axis=1, keepdims=True
        )
        distance = own_squares + row_squares - 2.0 * row_gram
        divisor = jnp.full((piece, count), scale * total_cells, jnp.float32)
        krows[half, me] = jnp.exp(-distance / divisor).astype(jnp.bfloat16)
        for k in range(1, peers):
            k_copy(half, (me + k) % peers, me, k).start()

    def rs_start(inner):
        for k in range(1, peers):
            rs_copy((me + k) % peers, me, k, inner).start()

    def rs_finish(inner):
        for k in range(1, peers):
            source = (me + peers - k) % peers
            rs_copy(source, source, k, inner).wait_recv()
        span = slice(0, 2 * piece + 8 if inner else piece)
        inbox[me, span] = part[me, span]
        total = inbox[0, span]
        for k in range(1, peers):
            total = total + inbox[k, span]
        return total

    @pl.when(is_end)
    def _():
        rs_start(False)
        chain_step(1, 1)
        total = rs_finish(False)
        swap_out[:piece] = total
        swap(False).start()
        swap(True).wait_recv()
        make_rows(0, z, total + swap_in[:piece], swap_in[piece:piece + 1])
        chain_step(1, 2)

    @pl.when(is_inner)
    def _():
        rs_start(True)
        chain_step(1, 1)
        total = rs_finish(True)
        swap_out[...] = total[piece:]
        swap(True).start()
        make_rows(0, z, total[:piece], total[2 * piece:2 * piece + 1])
        chain_step(1, 2)
        swap(False).wait_recv()
        make_rows(1, mate, total[piece:2 * piece] + swap_in[:piece], total[2 * piece:2 * piece + 1])

    def k_wait(half):
        for k in range(1, peers):
            source = (me + peers - k) % peers
            k_copy(half, source, source, k).wait_recv()

    def rowsum_of(kernel):
        return jnp.sum(kernel.astype(jnp.float32), axis=1, keepdims=True)

    def pulled_term(kernel, level, field, far):
        own = one(level, field, far).astype(jnp.float32)
        pulled = jnp.dot(kernel, every(m_all, field, far), preferred_element_type=jnp.float32)
        factor = 2.0 / jnp.full(own.shape, scale, jnp.float32)
        return factor * (rowsum_of(kernel) * own - pulled)

    def attract_term(kernel, field, far):
        return jnp.dot(kernel, every(g_all, field, far), preferred_element_type=jnp.float32)

    k_wait(0)
    kernel = krows[0].reshape(slab, count)
    for field in range(fields):
        base[field, :, :held] = pulled_term(kernel, z, field, False)

    @pl.when(is_inner)
    def _():
        k_wait(1)
        mine = krows[0].reshape(slab, count)
        theirs = krows[1].reshape(slab, count)
        for field in range(fields):
            base[field, :, held:] = pulled_term(mine, z, field, True)
            base_far[field] = pulled_term(theirs, mate, field, True)

    chain_step(1, 3)

    def far_copy(field, to, source):
        return pltpu.make_async_remote_copy(
            src_ref=outbox_far.at[field, to],
            dst_ref=out_ref.at[field, :, columns(source, held, spare)],
            send_sem=o_send.at[1, field, to],
            recv_sem=o_recv.at[1, field, source],
            device_id=(mate * group + to, y),
            device_id_type=MESH,
        )

    def out_copy(field, to, source, inner):
        size = cells if inner else held
        return pltpu.make_async_remote_copy(
            src_ref=outbox.at[field, to, :, pl.ds(0, size)],
            dst_ref=out_ref.at[field, :, columns(source, 0, size)],
            send_sem=o_send.at[0, field, to],
            recv_sem=o_recv.at[0, field, source],
            device_id=(z * group + to, y),
            device_id_type=MESH,
        )

    for field in range(fields):
        @pl.when(is_inner)
        def _():
            mine = krows[0].reshape(slab, count)
            theirs = krows[1].reshape(slab, count)
            update = (attract_term(theirs, field, True) + base_far[field]) * (1.0 / count)
            outbox_far[field] = update.reshape(group, rows, spare)
            for to in range(group):
                far_copy(field, to, g).start()
            update = (attract_term(mine, field, True) + base[field, :, held:]) * (1.0 / count)
            outbox[field, :, :, held:] = update.reshape(group, rows, spare)

        update = (attract_term(kernel, field, False) + base[field, :, :held]) * (1.0 / count)
        outbox[field, :, :, :held] = update.reshape(group, rows, held)

        @pl.when(is_inner)
        def _():
            for k in range(1, group):
                out_copy(field, (g + k) % group, g, True).start()
            out_ref[field, :, columns(g)] = outbox[field, g]

        @pl.when(is_end)
        def _():
            for k in range(1, group):
                out_copy(field, (g + k) % group, g, False).start()
            out_ref[field, :, columns(g, 0, held)] = outbox[field, g, :, :held]

    chain_drain(0)
    chain_drain(1)
    for copy in pending:
        copy.wait_send()

    @pl.when(is_inner)
    def _():
        for k in range(1, peers):
            rs_copy((me + k) % peers, me, k, True).wait_send()
            k_copy(0, (me + k) % peers, me, k).wait_send()
            k_copy(1, (me + k) % peers, me, k).wait_send()
        swap(True).wait_send()
        for field in range(fields):
            for k in range(1, group):
                out_copy(field, (g + k) % group, g, True).wait_send()
                source = (g + group - k) % group
                out_copy(field, source, source, True).wait_recv()
            for to in range(group):
                far_copy(field, to, g).wait_send()

    @pl.when(is_end)
    def _():
        for k in range(1, peers):
            rs_copy((me + k) % peers, me, k, False).wait_send()
            k_copy(0, (me + k) % peers, me, k).wait_send()
        swap(False).wait_send()
        for field in range(fields):
            for k in range(1, group):
                out_copy(field, (g + k) % group, g, False).wait_send()
                source = (g + group - k) % group
                out_copy(field, source, source, False).wait_recv()
            for source in range(group):
                far_copy(field, source, source).wait_recv()


def fused_body(layers, group, planes, models, gradients, length_scale):
    fields, rows, width = models.shape
    cells = width // group
    slab = group * rows
    count = layers * slab
    peers = group * planes
    piece = slab // peers
    held = cells * 3 // 4
    dma = pltpu.SemaphoreType.DMA
    return pl.pallas_call(
        functools.partial(stein_kernel, layers, group, planes, held),
        out_shape=jax.ShapeDtypeStruct(models.shape, jnp.float32),
        in_specs=[
            pl.BlockSpec(memory_space=pltpu.SMEM),
            pl.BlockSpec(memory_space=pl.ANY),
            pl.BlockSpec(memory_space=pl.ANY),
        ],
        out_specs=pl.BlockSpec(memory_space=pltpu.VMEM),
        scratch_shapes=[
            pltpu.VMEM((layers, group, fields, rows, cells), jnp.bfloat16),
            pltpu.VMEM((layers, group, fields, rows, cells), jnp.bfloat16),
            pltpu.VMEM((peers, 2 * piece + 8, count), jnp.float32),
            pltpu.VMEM((peers, 2 * piece + 8, count), jnp.float32),
            pltpu.VMEM((piece + 8, count), jnp.float32),
            pltpu.VMEM((piece + 8, count), jnp.float32),
            pltpu.VMEM((2, peers, piece, count), jnp.bfloat16),
            pltpu.VMEM((fields, slab, cells), jnp.float32),
            pltpu.VMEM((fields, slab, cells - held), jnp.float32),
            pltpu.VMEM((fields, group, rows, cells), jnp.float32),
            pltpu.VMEM((fields, group, rows, cells - held), jnp.float32),
            dma((2,)),
            dma((2, group)),
            dma((layers, group)),
            dma((layers, group)),
            dma((2, 2, layers, group)),
            dma((peers,)),
            dma((peers,)),
            dma((2,)),
            dma((2, peers)),
            dma((2, peers)),
            dma((2, fields, group)),
            dma((2, fields, group)),
        ],
        compiler_params=pltpu.CompilerParams(collective_id=0, has_side_effects=True),
        name="stein",
    )(length_scale, models, gradients)


def solution(mesh):
    spread, planes = mesh.shape["dom"], mesh.shape["cell"]
    layers = math.isqrt(spread)
    group = spread // layers

    def body(models, gradients, length_scale):
        _, rows, width = models.shape
        fits = (
            layers == 4
            and layers * group == spread
            and width % (group * 512) == 0
            and rows % 16 == 0
            and (group * rows) % (group * planes * 16) == 0
        )
        if not fits:
            return plain_body(models, gradients, length_scale)
        return fused_body(layers, group, planes, models, gradients, length_scale)

    placed = (P(None, "dom", "cell"), P(None, "dom", "cell"), P())
    return jax.shard_map(
        body, mesh=mesh, in_specs=placed, out_specs=P(None, "dom", "cell"), check_vma=False
    )
```

```python
import functools
import math

import jax
import jax.numpy as jnp
from jax import lax
from jax.experimental import pallas as pl
from jax.experimental.pallas import tpu as pltpu
from jax.sharding import PartitionSpec as P

MESH = pl.DeviceIdType.MESH


def plain_body(models, gradients, length_scale):
    local_models, local_grads = (
        lax.all_to_all(models, "dom", split_axis=2, concat_axis=1, tiled=True),
        lax.all_to_all(gradients, "dom", split_axis=2, concat_axis=1, tiled=True),
    )
    cell_block = local_models.shape[2]
    particles = local_models.shape[1]
    cell_count = cell_block * lax.axis_size("dom") * lax.axis_size("cell")
    scale_value = length_scale[0]
    divisor = scale_value * cell_count
    partial_value = jnp.einsum(
        "kpc,kqc->pq", local_models, local_models, preferred_element_type=jnp.float32
    )
    summed = lax.psum(partial_value, "cell")
    row_block = lax.psum_scatter(summed, "dom", scatter_dimension=0, tiled=True)
    row_count = row_block.shape[0]
    row_start = lax.axis_index("dom") * row_count
    own_squares = jnp.diagonal(lax.dynamic_slice_in_dim(row_block, row_start, row_count, 1))
    squares = lax.all_gather(own_squares, "dom", axis=0, tiled=True)
    distance = own_squares[:, None] + squares[None, :] - 2.0 * row_block
    kernel = lax.all_gather(
        jnp.exp(-distance / divisor).astype(jnp.bfloat16), "dom", axis=0, tiled=True
    )
    rowsum = jnp.sum(kernel.astype(jnp.float32), axis=1)
    stacked = jnp.concatenate((local_grads, local_models), axis=2)
    product = jnp.einsum("pq,kqc->kpc", kernel, stacked, preferred_element_type=jnp.float32)
    attract = product[:, :, :cell_block]
    pulled = product[:, :, cell_block:]
    update = (
        attract
        + 2.0 / scale_value * (rowsum[None, :, None] * local_models.astype(jnp.float32) - pulled)
    ) / particles
    return lax.all_to_all(update, "dom", split_axis=1, concat_axis=2, tiled=True)


def stein_kernel(
    layers, group, planes, held,
    scale_ref, models_ref, grads_ref, out_ref,
    m_all, g_all, part, inbox, swap_out, swap_in, krows, base, base_far, outbox, outbox_far,
    local_sem, a2a_send, m_recv, g_recv, fwd_send,
    rs_send, rs_recv, swap_sem, k_send, k_recv, o_send, o_recv,
):
    fields, rows, width = models_ref.shape
    cells = width // group
    slab = group * rows
    count = layers * slab
    peers = group * planes
    piece = slab // peers
    total_cells = width * planes
    spare = cells - held
    near = pl.ds(0, held)
    dom = lax.axis_index("dom")
    y = lax.axis_index("cell")
    z = dom // group
    g = dom % group
    me = g * planes + y
    has_up = z + 1 < layers
    has_down = z > 0
    is_end = jnp.logical_or(z == 0, z == layers - 1)
    is_inner = jnp.logical_and(z > 0, z < layers - 1)
    mate = z + 1 - 2 * (z % 2)
    up_end = z + 1 == layers - 1
    down_end = z - 1 == 0

    def both(left, right):
        return jnp.logical_and(left, right)

    def columns(which, start=0, size=None):
        return pl.ds(pl.multiple_of(which * cells + start, 128), cells if size is None else size)

    def layer_id(which):
        return (z * group + which // planes, which % planes)

    barrier = pltpu.get_barrier_semaphore()
    for k in range(1, peers):
        pl.semaphore_signal(
            barrier, inc=1, device_id=layer_id((me + k) % peers), device_id_type=MESH
        )
    for k in range(1, group):
        pl.semaphore_signal(
            barrier,
            inc=1,
            device_id=(mate * group + (g + k) % group, y),
            device_id_type=MESH,
        )

    @pl.when(has_up)
    def _():
        pl.semaphore_signal(barrier, inc=1, device_id=(dom + group, y), device_id_type=MESH)

    @pl.when(has_down)
    def _():
        pl.semaphore_signal(barrier, inc=1, device_id=(dom - group, y), device_id_type=MESH)

    tensors = ((models_ref, m_all, m_recv), (grads_ref, g_all, g_recv))
    locals_ = []
    for t, (src, dst, _) in enumerate(tensors):
        copy = pltpu.make_async_copy(
            src.at[:, :, columns(g)], dst.at[z, g], local_sem.at[t]
        )
        copy.start()
        locals_.append(copy)

    neighbours = jnp.where(has_up, 1, 0) + jnp.where(has_down, 1, 0)
    pl.semaphore_wait(barrier, peers - 1 + group - 1 + neighbours)

    pending = []
    for t, (src, dst, recv) in enumerate(tensors):
        for k in range(1, group):
            to = (g + k) % group
            copy = pltpu.make_async_remote_copy(
                src_ref=src.at[:, :, columns(to)],
                dst_ref=dst.at[z, g],
                send_sem=a2a_send.at[t, k],
                recv_sem=recv.at[z, g],
                device_id=(z * group + to, y),
                device_id_type=MESH,
            )
            copy.start()
            pending.append(copy)

    def hop(t, up, level, which, step, k, short):
        _, buf, recv = tensors[t]
        block = buf.at[level, which, :, :, near] if short else buf.at[level, which]
        return pltpu.make_async_remote_copy(
            src_ref=block,
            dst_ref=block,
            send_sem=fwd_send.at[t, up, step, k],
            recv_sem=recv.at[level, which],
            device_id=(dom + group if up else dom - group, y),
            device_id_type=MESH,
        )

    def push(t, up, level, which, step, k, verb):
        exists, short = (has_up, up_end) if up else (has_down, down_end)

        @pl.when(both(exists, short))
        def _():
            getattr(hop(t, up, level, which, step, k, True), verb)()

        @pl.when(both(exists, jnp.logical_not(short)))
        def _():
            getattr(hop(t, up, level, which, step, k, False), verb)()

    def chain_step(t, step):
        for k in range(group):
            which = (g + group - k) % group
            if step == 0:
                if k == 0:
                    locals_[t].wait()
                else:
                    hop(t, 1, z, which, step, k, False).wait_recv()
                push(t, 1, z, which, step, k, "start")
                push(t, 0, z, which, step, k, "start")
                continue

            @pl.when(z >= step)
            def _():
                @pl.when(is_end)
                def _():
                    hop(t, 1, z - step, which, step, k, True).wait_recv()

                @pl.when(is_inner)
                def _():
                    hop(t, 1, z - step, which, step, k, False).wait_recv()

                push(t, 1, z - step, which, step, k, "start")

            @pl.when(z + step < layers)
            def _():
                @pl.when(is_end)
                def _():
                    hop(t, 0, z + step, which, step, k, True).wait_recv()

                @pl.when(is_inner)
                def _():
                    hop(t, 0, z + step, which, step, k, False).wait_recv()

                push(t, 0, z + step, which, step, k, "start")

    def chain_drain(t):
        for step in range(layers):
            for k in range(group):
                which = (g + group - k) % group

                @pl.when(z >= step)
                def _():
                    push(t, 1, z - step, which, step, k, "wait_send")

                @pl.when(z + step < layers)
                def _():
                    push(t, 0, z + step, which, step, k, "wait_send")

    def every(buf, field, far):
        if far:
            return buf[:, :, field, :, held:].reshape(count, spare)
        return buf[:, :, field, :, :held].reshape(count, held)

    def one(level, field, far):
        if far:
            return m_all[level, :, field, :, held:].reshape(slab, spare)
        return m_all[level, :, field, :, :held].reshape(slab, held)

    contract = (((1,), (1,)), ((), ()))

    def inner_product(left, right):
        return lax.dot_general(left, right, contract, preferred_element_type=jnp.float32)

    def block_of(buf, level, field, far):
        if far:
            return buf[level, :, field, :, held:].reshape(slab, spare)
        return buf[level, :, field, :, :held].reshape(slab, held)

    def rs_copy(level, to, slot, k, inner):
        span = pl.ds(0, 2 * piece + 8 if inner else piece)
        return pltpu.make_async_remote_copy(
            src_ref=part.at[level, to, span],
            dst_ref=inbox.at[level, slot, span],
            send_sem=rs_send.at[level, k],
            recv_sem=rs_recv.at[level, slot],
            device_id=layer_id(to),
            device_id_type=MESH,
        )

    def gram_level(level):
        own = jnp.zeros((slab, slab), jnp.float32)
        for field in range(fields):
            own += inner_product(one(z, field, False), block_of(m_all, level, field, False))
        part[level, :, :piece, :] = own.reshape(peers, piece, slab)

        @pl.when(is_inner)
        def _():
            mine = jnp.zeros((slab, slab), jnp.float32)
            other = jnp.zeros((slab, slab), jnp.float32)
            squares = jnp.zeros((8, slab), jnp.float32)
            for field in range(fields):
                far = block_of(m_all, level, field, True)
                mine += inner_product(one(z, field, True), far)
                other += inner_product(one(mate, field, True), far)
                for block in (block_of(m_all, level, field, False), far):
                    ones = jnp.ones((8, block.shape[1]), jnp.bfloat16)
                    wide = block.astype(jnp.float32)
                    wide = wide * wide
                    high = wide.astype(jnp.bfloat16)
                    low = (wide - high.astype(jnp.float32)).astype(jnp.bfloat16)
                    squares += inner_product(ones, high)
                    squares += inner_product(ones, low)
            part[level, :, :piece, :] += mine.reshape(peers, piece, slab)
            part[level, :, piece:2 * piece, :] = other.reshape(peers, piece, slab)
            part[level, :, 2 * piece:, :] = jnp.broadcast_to(squares[None], (peers, 8, slab))
            for k in range(1, peers):
                rs_copy(level, (me + k) % peers, me, k, True).start()
            inbox[level, me] = part[level, me]

        @pl.when(is_end)
        def _():
            for k in range(1, peers):
                rs_copy(level, (me + k) % peers, me, k, False).start()
            inbox[level, me, :piece] = part[level, me, :piece]

    def gram_step(step):
        @pl.when(z >= step)
        def _():
            gram_level(z - step)

        @pl.when(z + step < layers)
        def _():
            gram_level(z + step)

    chain_step(0, 0)

    @pl.when(is_end)
    def _():
        chain_step(1, 0)

    chain_step(0, 1)
    gram_level(z)
    gram_step(1)
    chain_step(0, 2)

    @pl.when(is_inner)
    def _():
        chain_step(1, 0)

    gram_step(2)
    chain_step(0, 3)
    gram_step(3)

    def swap(inner):
        span = pl.ds(0, piece + 8 if inner else piece)
        return pltpu.make_async_remote_copy(
            src_ref=swap_out.at[span],
            dst_ref=swap_in.at[span],
            send_sem=swap_sem.at[0],
            recv_sem=swap_sem.at[1],
            device_id=(mate * group + g, y),
            device_id_type=MESH,
        )

    def k_copy(half, to, slot, k):
        return pltpu.make_async_remote_copy(
            src_ref=krows.at[half, slot],
            dst_ref=krows.at[half, slot],
            send_sem=k_send.at[half, k],
            recv_sem=k_recv.at[half, slot],
            device_id=layer_id(to),
            device_id_type=MESH,
        )

    scale = scale_ref[0]

    def make_rows(half, level, row_gram, row_squares):
        first = level * slab + me * piece
        row_index = lax.broadcasted_iota(jnp.int32, (piece, count), 0) + first
        col_index = lax.broadcasted_iota(jnp.int32, (piece, count), 1)
        own_squares = jnp.sum(
            jnp.where(row_index == col_index, row_gram, 0.0), axis=1, keepdims=True
        )
        distance = own_squares + row_squares - 2.0 * row_gram
        divisor = jnp.full((piece, count), scale * total_cells, jnp.float32)
        krows[half, me] = jnp.exp(-distance / divisor).astype(jnp.bfloat16)
        for k in range(1, peers):
            k_copy(half, (me + k) % peers, me, k).start()

    def rs_finish(inner):
        span = slice(0, 2 * piece + 8 if inner else piece)
        totals = []
        for level in range(layers):
            for k in range(1, peers):
                source = (me + peers - k) % peers
                rs_copy(level, source, source, k, inner).wait_recv()
            total = inbox[level, 0, span]
            for k in range(1, peers):
                total = total + inbox[level, k, span]
            totals.append(total)
        return jnp.concatenate(totals, axis=1)

    @pl.when(is_end)
    def _():
        chain_step(1, 1)
        total = rs_finish(False)
        swap_out[:piece] = total
        swap(False).start()
        swap(True).wait_recv()
        make_rows(0, z, total + swap_in[:piece], swap_in[piece:piece + 1])
        chain_step(1, 2)

    @pl.when(is_inner)
    def _():
        chain_step(1, 1)
        total = rs_finish(True)
        swap_out[...] = total[piece:]
        swap(True).start()
        make_rows(0, z, total[:piece], total[2 * piece:2 * piece + 1])
        chain_step(1, 2)
        swap(False).wait_recv()
        make_rows(1, mate, total[piece:2 * piece] + swap_in[:piece], total[2 * piece:2 * piece + 1])

    def k_wait(half):
        for k in range(1, peers):
            source = (me + peers - k) % peers
            k_copy(half, source, source, k).wait_recv()

    def rowsum_of(kernel):
        return jnp.sum(kernel.astype(jnp.float32), axis=1, keepdims=True)

    def pulled_term(kernel, level, field, far):
        own = one(level, field, far).astype(jnp.float32)
        pulled = jnp.dot(kernel, every(m_all, field, far), preferred_element_type=jnp.float32)
        factor = 2.0 / jnp.full(own.shape, scale, jnp.float32)
        return factor * (rowsum_of(kernel) * own - pulled)

    def attract_term(kernel, field, far):
        return jnp.dot(kernel, every(g_all, field, far), preferred_element_type=jnp.float32)

    k_wait(0)
    kernel = krows[0].reshape(slab, count)
    for field in range(fields):
        base[field, :, :held] = pulled_term(kernel, z, field, False)

    @pl.when(is_inner)
    def _():
        k_wait(1)
        mine = krows[0].reshape(slab, count)
        theirs = krows[1].reshape(slab, count)
        for field in range(fields):
            base[field, :, held:] = pulled_term(mine, z, field, True)
            base_far[field] = pulled_term(theirs, mate, field, True)

    chain_step(1, 3)

    def far_copy(field, to, source):
        return pltpu.make_async_remote_copy(
            src_ref=outbox_far.at[field, to],
            dst_ref=out_ref.at[field, :, columns(source, held, spare)],
            send_sem=o_send.at[1, field, to],
            recv_sem=o_recv.at[1, field, source],
            device_id=(mate * group + to, y),
            device_id_type=MESH,
        )

    def out_copy(field, to, source, inner):
        size = cells if inner else held
        return pltpu.make_async_remote_copy(
            src_ref=outbox.at[field, to, :, pl.ds(0, size)],
            dst_ref=out_ref.at[field, :, columns(source, 0, size)],
            send_sem=o_send.at[0, field, to],
            recv_sem=o_recv.at[0, field, source],
            device_id=(z * group + to, y),
            device_id_type=MESH,
        )

    for field in range(fields):
        @pl.when(is_inner)
        def _():
            mine = krows[0].reshape(slab, count)
            theirs = krows[1].reshape(slab, count)
            update = (attract_term(theirs, field, True) + base_far[field]) * (1.0 / count)
            outbox_far[field] = update.reshape(group, rows, spare)
            for to in range(group):
                far_copy(field, to, g).start()
            update = (attract_term(mine, field, True) + base[field, :, held:]) * (1.0 / count)
            outbox[field, :, :, held:] = update.reshape(group, rows, spare)

        update = (attract_term(kernel, field, False) + base[field, :, :held]) * (1.0 / count)
        outbox[field, :, :, :held] = update.reshape(group, rows, held)

        @pl.when(is_inner)
        def _():
            for k in range(1, group):
                out_copy(field, (g + k) % group, g, True).start()
            out_ref[field, :, columns(g)] = outbox[field, g]

        @pl.when(is_end)
        def _():
            for k in range(1, group):
                out_copy(field, (g + k) % group, g, False).start()
            out_ref[field, :, columns(g, 0, held)] = outbox[field, g, :, :held]

    chain_drain(0)
    chain_drain(1)
    for copy in pending:
        copy.wait_send()

    @pl.when(is_inner)
    def _():
        for k in range(1, peers):
            for level in range(layers):
                rs_copy(level, (me + k) % peers, me, k, True).wait_send()
            k_copy(0, (me + k) % peers, me, k).wait_send()
            k_copy(1, (me + k) % peers, me, k).wait_send()
        swap(True).wait_send()
        for field in range(fields):
            for k in range(1, group):
                out_copy(field, (g + k) % group, g, True).wait_send()
                source = (g + group - k) % group
                out_copy(field, source, source, True).wait_recv()
            for to in range(group):
                far_copy(field, to, g).wait_send()

    @pl.when(is_end)
    def _():
        for k in range(1, peers):
            for level in range(layers):
                rs_copy(level, (me + k) % peers, me, k, False).wait_send()
            k_copy(0, (me + k) % peers, me, k).wait_send()
        swap(False).wait_send()
        for field in range(fields):
            for k in range(1, group):
                out_copy(field, (g + k) % group, g, False).wait_send()
                source = (g + group - k) % group
                out_copy(field, source, source, False).wait_recv()
            for source in range(group):
                far_copy(field, source, source).wait_recv()


def fused_body(layers, group, planes, models, gradients, length_scale):
    fields, rows, width = models.shape
    cells = width // group
    slab = group * rows
    count = layers * slab
    peers = group * planes
    piece = slab // peers
    held = cells // 2
    dma = pltpu.SemaphoreType.DMA
    return pl.pallas_call(
        functools.partial(stein_kernel, layers, group, planes, held),
        out_shape=jax.ShapeDtypeStruct(models.shape, jnp.float32),
        in_specs=[
            pl.BlockSpec(memory_space=pltpu.SMEM),
            pl.BlockSpec(memory_space=pl.ANY),
            pl.BlockSpec(memory_space=pl.ANY),
        ],
        out_specs=pl.BlockSpec(memory_space=pltpu.VMEM),
        scratch_shapes=[
            pltpu.VMEM((layers, group, fields, rows, cells), jnp.bfloat16),
            pltpu.VMEM((layers, group, fields, rows, cells), jnp.bfloat16),
            pltpu.VMEM((layers, peers, 2 * piece + 8, slab), jnp.float32),
            pltpu.VMEM((layers, peers, 2 * piece + 8, slab), jnp.float32),
            pltpu.VMEM((piece + 8, count), jnp.float32),
            pltpu.VMEM((piece + 8, count), jnp.float32),
            pltpu.VMEM((2, peers, piece, count), jnp.bfloat16),
            pltpu.VMEM((fields, slab, cells), jnp.float32),
            pltpu.VMEM((fields, slab, cells - held), jnp.float32),
            pltpu.VMEM((fields, group, rows, cells), jnp.float32),
            pltpu.VMEM((fields, group, rows, cells - held), jnp.float32),
            dma((2,)),
            dma((2, group)),
            dma((layers, group)),
            dma((layers, group)),
            dma((2, 2, layers, group)),
            dma((layers, peers)),
            dma((layers, peers)),
            dma((2,)),
            dma((2, peers)),
            dma((2, peers)),
            dma((2, fields, group)),
            dma((2, fields, group)),
        ],
        compiler_params=pltpu.CompilerParams(collective_id=0, has_side_effects=True),
        name="stein",
    )(length_scale, models, gradients)


def solution(mesh):
    spread, planes = mesh.shape["dom"], mesh.shape["cell"]
    layers = math.isqrt(spread)
    group = spread // layers

    def body(models, gradients, length_scale):
        _, rows, width = models.shape
        fits = (
            layers == 4
            and layers * group == spread
            and width % (group * 512) == 0
            and rows % 16 == 0
            and (group * rows) % 128 == 0
            and (group * rows) % (group * planes * 16) == 0
        )
        if not fits:
            return plain_body(models, gradients, length_scale)
        return fused_body(layers, group, planes, models, gradients, length_scale)

    placed = (P(None, "dom", "cell"), P(None, "dom", "cell"), P())
    return jax.shard_map(
        body, mesh=mesh, in_specs=placed, out_specs=P(None, "dom", "cell"), check_vma=False
    )
```

```python
import functools
import math

import jax
import jax.numpy as jnp
from jax import lax
from jax.experimental import pallas as pl
from jax.experimental.pallas import tpu as pltpu
from jax.sharding import PartitionSpec as P

MESH = pl.DeviceIdType.MESH


def plain_body(models, gradients, length_scale):
    local_models, local_grads = (
        lax.all_to_all(models, "dom", split_axis=2, concat_axis=1, tiled=True),
        lax.all_to_all(gradients, "dom", split_axis=2, concat_axis=1, tiled=True),
    )
    cell_block = local_models.shape[2]
    particles = local_models.shape[1]
    cell_count = cell_block * lax.axis_size("dom") * lax.axis_size("cell")
    scale_value = length_scale[0]
    divisor = scale_value * cell_count
    partial_value = jnp.einsum(
        "kpc,kqc->pq", local_models, local_models, preferred_element_type=jnp.float32
    )
    summed = lax.psum(partial_value, "cell")
    row_block = lax.psum_scatter(summed, "dom", scatter_dimension=0, tiled=True)
    row_count = row_block.shape[0]
    row_start = lax.axis_index("dom") * row_count
    own_squares = jnp.diagonal(lax.dynamic_slice_in_dim(row_block, row_start, row_count, 1))
    squares = lax.all_gather(own_squares, "dom", axis=0, tiled=True)
    distance = own_squares[:, None] + squares[None, :] - 2.0 * row_block
    kernel = lax.all_gather(
        jnp.exp(-distance / divisor).astype(jnp.bfloat16), "dom", axis=0, tiled=True
    )
    rowsum = jnp.sum(kernel.astype(jnp.float32), axis=1)
    stacked = jnp.concatenate((local_grads, local_models), axis=2)
    product = jnp.einsum("pq,kqc->kpc", kernel, stacked, preferred_element_type=jnp.float32)
    attract = product[:, :, :cell_block]
    pulled = product[:, :, cell_block:]
    update = (
        attract
        + 2.0 / scale_value * (rowsum[None, :, None] * local_models.astype(jnp.float32) - pulled)
    ) / particles
    return lax.all_to_all(update, "dom", split_axis=1, concat_axis=2, tiled=True)


def stein_kernel(
    layers, group, planes, held,
    scale_ref, models_ref, grads_ref, out_ref,
    m_all, g_zero, g_one, part, inbox, swap_out, swap_in, krows, base, base_far, outbox, outbox_far,
    local_sem, a2a_send, chain_recv, fwd_send,
    rs_send, rs_recv, swap_sem, k_send, k_recv, o_send, o_recv,
):
    fields, rows, width = models_ref.shape
    cells = width // group
    slab = group * rows
    count = layers * slab
    peers = group * planes
    piece = slab // peers
    total_cells = width * planes
    spare = cells - held
    near = pl.ds(0, held)
    dom = lax.axis_index("dom")
    y = lax.axis_index("cell")
    z = dom // group
    g = dom % group
    me = g * planes + y
    has_up = z + 1 < layers
    has_down = z > 0
    is_end = jnp.logical_or(z == 0, z == layers - 1)
    is_inner = jnp.logical_and(z > 0, z < layers - 1)
    mate = z + 1 - 2 * (z % 2)
    up_end = z + 1 == layers - 1
    down_end = z - 1 == 0

    def both(left, right):
        return jnp.logical_and(left, right)

    def columns(which, start=0, size=None):
        return pl.ds(pl.multiple_of(which * cells + start, 128), cells if size is None else size)

    def layer_id(which):
        return (z * group + which // planes, which % planes)

    barrier = pltpu.get_barrier_semaphore()
    for k in range(1, peers):
        pl.semaphore_signal(
            barrier, inc=1, device_id=layer_id((me + k) % peers), device_id_type=MESH
        )
    for k in range(1, group):
        pl.semaphore_signal(
            barrier,
            inc=1,
            device_id=(mate * group + (g + k) % group, y),
            device_id_type=MESH,
        )

    @pl.when(has_up)
    def _():
        pl.semaphore_signal(barrier, inc=1, device_id=(dom + group, y), device_id_type=MESH)

    @pl.when(has_down)
    def _():
        pl.semaphore_signal(barrier, inc=1, device_id=(dom - group, y), device_id_type=MESH)

    tensors = (
        (models_ref, m_all, chain_recv.at[0]),
        (grads_ref.at[0], g_zero, chain_recv.at[1]),
        (grads_ref.at[1], g_one, chain_recv.at[2]),
    )

    def strip(ref, span):
        if len(ref.shape) == 3:
            return ref.at[:, :, span]
        return ref.at[:, span]

    locals_ = []
    for t, (src, dst, _) in enumerate(tensors):
        copy = pltpu.make_async_copy(
            strip(src, columns(g)), dst.at[z, g], local_sem.at[t]
        )
        copy.start()
        locals_.append(copy)

    neighbours = jnp.where(has_up, 1, 0) + jnp.where(has_down, 1, 0)
    pl.semaphore_wait(barrier, peers - 1 + group - 1 + neighbours)

    pending = []
    for t, (src, dst, recv) in enumerate(tensors):
        for k in range(1, group):
            to = (g + k) % group
            copy = pltpu.make_async_remote_copy(
                src_ref=strip(src, columns(to)),
                dst_ref=dst.at[z, g],
                send_sem=a2a_send.at[t, k],
                recv_sem=recv.at[z, g],
                device_id=(z * group + to, y),
                device_id_type=MESH,
            )
            copy.start()
            pending.append(copy)

    def hop(t, up, level, which, step, k, short):
        _, buf, recv = tensors[t]
        block = strip(buf.at[level, which], near) if short else buf.at[level, which]
        return pltpu.make_async_remote_copy(
            src_ref=block,
            dst_ref=block,
            send_sem=fwd_send.at[t, up, step, k],
            recv_sem=recv.at[level, which],
            device_id=(dom + group if up else dom - group, y),
            device_id_type=MESH,
        )

    def push(t, up, level, which, step, k, verb):
        exists, short = (has_up, up_end) if up else (has_down, down_end)

        @pl.when(both(exists, short))
        def _():
            getattr(hop(t, up, level, which, step, k, True), verb)()

        @pl.when(both(exists, jnp.logical_not(short)))
        def _():
            getattr(hop(t, up, level, which, step, k, False), verb)()

    def chain_step(t, step):
        for k in range(group):
            which = (g + group - k) % group
            if step == 0:
                if k == 0:
                    locals_[t].wait()
                else:
                    hop(t, 1, z, which, step, k, False).wait_recv()
                push(t, 1, z, which, step, k, "start")
                push(t, 0, z, which, step, k, "start")
                continue

            @pl.when(z >= step)
            def _():
                @pl.when(is_end)
                def _():
                    hop(t, 1, z - step, which, step, k, True).wait_recv()

                @pl.when(is_inner)
                def _():
                    hop(t, 1, z - step, which, step, k, False).wait_recv()

                push(t, 1, z - step, which, step, k, "start")

            @pl.when(z + step < layers)
            def _():
                @pl.when(is_end)
                def _():
                    hop(t, 0, z + step, which, step, k, True).wait_recv()

                @pl.when(is_inner)
                def _():
                    hop(t, 0, z + step, which, step, k, False).wait_recv()

                push(t, 0, z + step, which, step, k, "start")

    def chain_drain(t):
        for step in range(layers):
            for k in range(group):
                which = (g + group - k) % group

                @pl.when(z >= step)
                def _():
                    push(t, 1, z - step, which, step, k, "wait_send")

                @pl.when(z + step < layers)
                def _():
                    push(t, 0, z + step, which, step, k, "wait_send")

    def every(buf, field, far):
        if far:
            return buf[:, :, field, :, held:].reshape(count, spare)
        return buf[:, :, field, :, :held].reshape(count, held)

    def one(level, field, far):
        if far:
            return m_all[level, :, field, :, held:].reshape(slab, spare)
        return m_all[level, :, field, :, :held].reshape(slab, held)

    contract = (((1,), (1,)), ((), ()))

    def inner_product(left, right):
        return lax.dot_general(left, right, contract, preferred_element_type=jnp.float32)

    def block_of(buf, level, field, far):
        if far:
            return buf[level, :, field, :, held:].reshape(slab, spare)
        return buf[level, :, field, :, :held].reshape(slab, held)

    def rs_copy(level, to, slot, k, inner):
        span = pl.ds(0, 2 * piece + 8 if inner else piece)
        return pltpu.make_async_remote_copy(
            src_ref=part.at[level, to, span],
            dst_ref=inbox.at[level, slot, span],
            send_sem=rs_send.at[level, k],
            recv_sem=rs_recv.at[level, slot],
            device_id=layer_id(to),
            device_id_type=MESH,
        )

    def gram_level(level):
        own = jnp.zeros((slab, slab), jnp.float32)
        for field in range(fields):
            own += inner_product(one(z, field, False), block_of(m_all, level, field, False))
        part[level, :, :piece, :] = own.reshape(peers, piece, slab)

        @pl.when(is_inner)
        def _():
            mine = jnp.zeros((slab, slab), jnp.float32)
            other = jnp.zeros((slab, slab), jnp.float32)
            squares = jnp.zeros((8, slab), jnp.float32)
            for field in range(fields):
                far = block_of(m_all, level, field, True)
                mine += inner_product(one(z, field, True), far)
                other += inner_product(one(mate, field, True), far)
                for block in (block_of(m_all, level, field, False), far):
                    ones = jnp.ones((8, block.shape[1]), jnp.bfloat16)
                    wide = block.astype(jnp.float32)
                    wide = wide * wide
                    high = wide.astype(jnp.bfloat16)
                    low = (wide - high.astype(jnp.float32)).astype(jnp.bfloat16)
                    squares += inner_product(ones, high)
                    squares += inner_product(ones, low)
            part[level, :, :piece, :] += mine.reshape(peers, piece, slab)
            part[level, :, piece:2 * piece, :] = other.reshape(peers, piece, slab)
            part[level, :, 2 * piece:, :] = jnp.broadcast_to(squares[None], (peers, 8, slab))
            for k in range(1, peers):
                rs_copy(level, (me + k) % peers, me, k, True).start()
            inbox[level, me] = part[level, me]

        @pl.when(is_end)
        def _():
            for k in range(1, peers):
                rs_copy(level, (me + k) % peers, me, k, False).start()
            inbox[level, me, :piece] = part[level, me, :piece]

    def gram_step(step):
        @pl.when(z >= step)
        def _():
            gram_level(z - step)

        @pl.when(z + step < layers)
        def _():
            gram_level(z + step)

    chain_step(0, 0)

    @pl.when(is_end)
    def _():
        chain_step(1, 0)
        chain_step(2, 0)

    chain_step(0, 1)
    gram_level(z)
    gram_step(1)
    chain_step(0, 2)

    @pl.when(is_inner)
    def _():
        chain_step(1, 0)

    gram_step(2)
    chain_step(0, 3)
    gram_step(3)

    def swap(inner):
        span = pl.ds(0, piece + 8 if inner else piece)
        return pltpu.make_async_remote_copy(
            src_ref=swap_out.at[span],
            dst_ref=swap_in.at[span],
            send_sem=swap_sem.at[0],
            recv_sem=swap_sem.at[1],
            device_id=(mate * group + g, y),
            device_id_type=MESH,
        )

    def k_copy(half, to, slot, k):
        return pltpu.make_async_remote_copy(
            src_ref=krows.at[half, slot],
            dst_ref=krows.at[half, slot],
            send_sem=k_send.at[half, k],
            recv_sem=k_recv.at[half, slot],
            device_id=layer_id(to),
            device_id_type=MESH,
        )

    scale = scale_ref[0]

    def make_rows(half, level, row_gram, row_squares):
        first = level * slab + me * piece
        row_index = lax.broadcasted_iota(jnp.int32, (piece, count), 0) + first
        col_index = lax.broadcasted_iota(jnp.int32, (piece, count), 1)
        own_squares = jnp.sum(
            jnp.where(row_index == col_index, row_gram, 0.0), axis=1, keepdims=True
        )
        distance = own_squares + row_squares - 2.0 * row_gram
        divisor = jnp.full((piece, count), scale * total_cells, jnp.float32)
        krows[half, me] = jnp.exp(-distance / divisor).astype(jnp.bfloat16)
        for k in range(1, peers):
            k_copy(half, (me + k) % peers, me, k).start()

    def rs_finish(inner):
        span = slice(0, 2 * piece + 8 if inner else piece)
        totals = []
        for level in range(layers):
            for k in range(1, peers):
                source = (me + peers - k) % peers
                rs_copy(level, source, source, k, inner).wait_recv()
            total = inbox[level, 0, span]
            for k in range(1, peers):
                total = total + inbox[level, k, span]
            totals.append(total)
        return jnp.concatenate(totals, axis=1)

    @pl.when(is_end)
    def _():
        total = rs_finish(False)
        swap_out[:piece] = total
        swap(False).start()
        swap(True).wait_recv()
        make_rows(0, z, total + swap_in[:piece], swap_in[piece:piece + 1])

    @pl.when(is_inner)
    def _():
        chain_step(1, 1)
        chain_step(2, 0)
        total = rs_finish(True)
        swap_out[...] = total[piece:]
        swap(True).start()
        make_rows(0, z, total[:piece], total[2 * piece:2 * piece + 1])
        chain_step(1, 2)
        swap(False).wait_recv()
        make_rows(1, mate, total[piece:2 * piece] + swap_in[:piece], total[2 * piece:2 * piece + 1])
        chain_step(2, 1)

    def k_wait(half):
        for k in range(1, peers):
            source = (me + peers - k) % peers
            k_copy(half, source, source, k).wait_recv()

    def rowsum_of(kernel):
        return jnp.sum(kernel.astype(jnp.float32), axis=1, keepdims=True)

    def pulled_term(kernel, level, field, far):
        own = one(level, field, far).astype(jnp.float32)
        pulled = jnp.dot(kernel, every(m_all, field, far), preferred_element_type=jnp.float32)
        factor = 2.0 / jnp.full(own.shape, scale, jnp.float32)
        return factor * (rowsum_of(kernel) * own - pulled)

    def attract_term(kernel, field, far):
        buf = (g_zero, g_one)[field]
        block = buf[..., held:] if far else buf[..., :held]
        block = block.reshape(count, block.shape[-1])
        return jnp.dot(kernel, block, preferred_element_type=jnp.float32)

    k_wait(0)
    kernel = krows[0].reshape(slab, count)
    for field in range(fields):
        base[field, :, :held] = pulled_term(kernel, z, field, False)

    @pl.when(is_inner)
    def _():
        k_wait(1)
        mine = krows[0].reshape(slab, count)
        theirs = krows[1].reshape(slab, count)
        for field in range(fields):
            base[field, :, held:] = pulled_term(mine, z, field, True)
            base_far[field] = pulled_term(theirs, mate, field, True)

    def far_copy(field, to, source):
        return pltpu.make_async_remote_copy(
            src_ref=outbox_far.at[field, to],
            dst_ref=out_ref.at[field, :, columns(source, held, spare)],
            send_sem=o_send.at[1, field, to],
            recv_sem=o_recv.at[1, field, source],
            device_id=(mate * group + to, y),
            device_id_type=MESH,
        )

    def out_copy(field, to, source, inner):
        size = cells if inner else held
        return pltpu.make_async_remote_copy(
            src_ref=outbox.at[field, to, :, pl.ds(0, size)],
            dst_ref=out_ref.at[field, :, columns(source, 0, size)],
            send_sem=o_send.at[0, field, to],
            recv_sem=o_recv.at[0, field, source],
            device_id=(z * group + to, y),
            device_id_type=MESH,
        )

    for field in range(fields):
        @pl.when(is_end)
        def _():
            for step in range(1, layers):
                chain_step(1 + field, step)

        if field == 1:
            @pl.when(is_inner)
            def _():
                chain_step(2, 2)

        @pl.when(is_inner)
        def _():
            mine = krows[0].reshape(slab, count)
            theirs = krows[1].reshape(slab, count)
            update = (attract_term(theirs, field, True) + base_far[field]) * (1.0 / count)
            outbox_far[field] = update.reshape(group, rows, spare)
            for to in range(group):
                far_copy(field, to, g).start()
            update = (attract_term(mine, field, True) + base[field, :, held:]) * (1.0 / count)
            outbox[field, :, :, held:] = update.reshape(group, rows, spare)

        update = (attract_term(kernel, field, False) + base[field, :, :held]) * (1.0 / count)
        outbox[field, :, :, :held] = update.reshape(group, rows, held)

        @pl.when(is_inner)
        def _():
            for k in range(1, group):
                out_copy(field, (g + k) % group, g, True).start()
            out_ref[field, :, columns(g)] = outbox[field, g]

        @pl.when(is_end)
        def _():
            for k in range(1, group):
                out_copy(field, (g + k) % group, g, False).start()
            out_ref[field, :, columns(g, 0, held)] = outbox[field, g, :, :held]

    chain_drain(0)
    chain_drain(1)
    chain_drain(2)
    for copy in pending:
        copy.wait_send()

    @pl.when(is_inner)
    def _():
        for k in range(1, peers):
            for level in range(layers):
                rs_copy(level, (me + k) % peers, me, k, True).wait_send()
            k_copy(0, (me + k) % peers, me, k).wait_send()
            k_copy(1, (me + k) % peers, me, k).wait_send()
        swap(True).wait_send()
        for field in range(fields):
            for k in range(1, group):
                out_copy(field, (g + k) % group, g, True).wait_send()
                source = (g + group - k) % group
                out_copy(field, source, source, True).wait_recv()
            for to in range(group):
                far_copy(field, to, g).wait_send()

    @pl.when(is_end)
    def _():
        for k in range(1, peers):
            for level in range(layers):
                rs_copy(level, (me + k) % peers, me, k, False).wait_send()
            k_copy(0, (me + k) % peers, me, k).wait_send()
        swap(False).wait_send()
        for field in range(fields):
            for k in range(1, group):
                out_copy(field, (g + k) % group, g, False).wait_send()
                source = (g + group - k) % group
                out_copy(field, source, source, False).wait_recv()
            for source in range(group):
                far_copy(field, source, source).wait_recv()


def fused_body(layers, group, planes, models, gradients, length_scale):
    fields, rows, width = models.shape
    cells = width // group
    slab = group * rows
    count = layers * slab
    peers = group * planes
    piece = slab // peers
    held = cells // 2
    dma = pltpu.SemaphoreType.DMA
    return pl.pallas_call(
        functools.partial(stein_kernel, layers, group, planes, held),
        out_shape=jax.ShapeDtypeStruct(models.shape, jnp.float32),
        in_specs=[
            pl.BlockSpec(memory_space=pltpu.SMEM),
            pl.BlockSpec(memory_space=pl.ANY),
            pl.BlockSpec(memory_space=pl.ANY),
        ],
        out_specs=pl.BlockSpec(memory_space=pltpu.VMEM),
        scratch_shapes=[
            pltpu.VMEM((layers, group, fields, rows, cells), jnp.bfloat16),
            pltpu.VMEM((layers, group, rows, cells), jnp.bfloat16),
            pltpu.VMEM((layers, group, rows, cells), jnp.bfloat16),
            pltpu.VMEM((layers, peers, 2 * piece + 8, slab), jnp.float32),
            pltpu.VMEM((layers, peers, 2 * piece + 8, slab), jnp.float32),
            pltpu.VMEM((piece + 8, count), jnp.float32),
            pltpu.VMEM((piece + 8, count), jnp.float32),
            pltpu.VMEM((2, peers, piece, count), jnp.bfloat16),
            pltpu.VMEM((fields, slab, cells), jnp.float32),
            pltpu.VMEM((fields, slab, cells - held), jnp.float32),
            pltpu.VMEM((fields, group, rows, cells), jnp.float32),
            pltpu.VMEM((fields, group, rows, cells - held), jnp.float32),
            dma((3,)),
            dma((3, group)),
            dma((3, layers, group)),
            dma((3, 2, layers, group)),
            dma((layers, peers)),
            dma((layers, peers)),
            dma((2,)),
            dma((2, peers)),
            dma((2, peers)),
            dma((2, fields, group)),
            dma((2, fields, group)),
        ],
        compiler_params=pltpu.CompilerParams(collective_id=0, has_side_effects=True),
        name="stein",
    )(length_scale, models, gradients)


def solution(mesh):
    spread, planes = mesh.shape["dom"], mesh.shape["cell"]
    layers = math.isqrt(spread)
    group = spread // layers

    def body(models, gradients, length_scale):
        _, rows, width = models.shape
        fits = (
            layers == 4
            and models.shape[0] == 2
            and layers * group == spread
            and width % (group * 512) == 0
            and rows % 16 == 0
            and (group * rows) % 128 == 0
            and (group * rows) % (group * planes * 16) == 0
        )
        if not fits:
            return plain_body(models, gradients, length_scale)
        return fused_body(layers, group, planes, models, gradients, length_scale)

    placed = (P(None, "dom", "cell"), P(None, "dom", "cell"), P())
    return jax.shard_map(
        body, mesh=mesh, in_specs=placed, out_specs=P(None, "dom", "cell"), check_vma=False
    )
```

```python
import functools
import math

import jax
import jax.numpy as jnp
from jax import lax
from jax.experimental import pallas as pl
from jax.experimental.pallas import tpu as pltpu
from jax.sharding import PartitionSpec as P

MESH = pl.DeviceIdType.MESH


def plain_body(models, gradients, length_scale):
    local_models, local_grads = (
        lax.all_to_all(models, "dom", split_axis=2, concat_axis=1, tiled=True),
        lax.all_to_all(gradients, "dom", split_axis=2, concat_axis=1, tiled=True),
    )
    cell_block = local_models.shape[2]
    particles = local_models.shape[1]
    cell_count = cell_block * lax.axis_size("dom") * lax.axis_size("cell")
    scale_value = length_scale[0]
    divisor = scale_value * cell_count
    partial_value = jnp.einsum(
        "kpc,kqc->pq", local_models, local_models, preferred_element_type=jnp.float32
    )
    summed = lax.psum(partial_value, "cell")
    row_block = lax.psum_scatter(summed, "dom", scatter_dimension=0, tiled=True)
    row_count = row_block.shape[0]
    row_start = lax.axis_index("dom") * row_count
    own_squares = jnp.diagonal(lax.dynamic_slice_in_dim(row_block, row_start, row_count, 1))
    squares = lax.all_gather(own_squares, "dom", axis=0, tiled=True)
    distance = own_squares[:, None] + squares[None, :] - 2.0 * row_block
    kernel = lax.all_gather(
        jnp.exp(-distance / divisor).astype(jnp.bfloat16), "dom", axis=0, tiled=True
    )
    rowsum = jnp.sum(kernel.astype(jnp.float32), axis=1)
    stacked = jnp.concatenate((local_grads, local_models), axis=2)
    product = jnp.einsum("pq,kqc->kpc", kernel, stacked, preferred_element_type=jnp.float32)
    attract = product[:, :, :cell_block]
    pulled = product[:, :, cell_block:]
    update = (
        attract
        + 2.0 / scale_value * (rowsum[None, :, None] * local_models.astype(jnp.float32) - pulled)
    ) / particles
    return lax.all_to_all(update, "dom", split_axis=1, concat_axis=2, tiled=True)


def stein_kernel(
    layers, group, planes, held,
    scale_ref, models_ref, grads_ref, out_ref,
    m_all, g_zero, g_one, part, inbox, swap_out, swap_in, krows, base, base_far, outbox, outbox_far,
    local_sem, a2a_send, chain_recv, fwd_send,
    rs_send, rs_recv, swap_sem, k_send, k_recv, o_send, o_recv,
):
    fields, rows, width = models_ref.shape
    cells = width // group
    slab = group * rows
    count = layers * slab
    peers = group * planes
    piece = slab // peers
    total_cells = width * planes
    spare = cells - held
    near = pl.ds(0, held)
    dom = lax.axis_index("dom")
    y = lax.axis_index("cell")
    z = dom // group
    g = dom % group
    me = g * planes + y
    has_up = z + 1 < layers
    has_down = z > 0
    is_end = jnp.logical_or(z == 0, z == layers - 1)
    is_inner = jnp.logical_and(z > 0, z < layers - 1)
    mate = z + 1 - 2 * (z % 2)
    up_end = z + 1 == layers - 1
    down_end = z - 1 == 0

    def both(left, right):
        return jnp.logical_and(left, right)

    def columns(which, start=0, size=None):
        return pl.ds(pl.multiple_of(which * cells + start, 128), cells if size is None else size)

    def layer_id(which):
        return (z * group + which // planes, which % planes)

    barrier = pltpu.get_barrier_semaphore()
    for k in range(1, peers):
        pl.semaphore_signal(
            barrier, inc=1, device_id=layer_id((me + k) % peers), device_id_type=MESH
        )
    for k in range(1, group):
        pl.semaphore_signal(
            barrier,
            inc=1,
            device_id=(mate * group + (g + k) % group, y),
            device_id_type=MESH,
        )

    @pl.when(has_up)
    def _():
        pl.semaphore_signal(barrier, inc=1, device_id=(dom + group, y), device_id_type=MESH)

    @pl.when(has_down)
    def _():
        pl.semaphore_signal(barrier, inc=1, device_id=(dom - group, y), device_id_type=MESH)

    tensors = (
        (models_ref, m_all, chain_recv.at[0]),
        (grads_ref.at[0], g_zero, chain_recv.at[1]),
        (grads_ref.at[1], g_one, chain_recv.at[2]),
    )

    def strip(ref, span):
        if len(ref.shape) == 3:
            return ref.at[:, :, span]
        return ref.at[:, span]

    locals_ = []
    for t, (src, dst, _) in enumerate(tensors):
        copy = pltpu.make_async_copy(
            strip(src, columns(g)), dst.at[z, g], local_sem.at[t]
        )
        copy.start()
        locals_.append(copy)

    neighbours = jnp.where(has_up, 1, 0) + jnp.where(has_down, 1, 0)
    pl.semaphore_wait(barrier, peers - 1 + group - 1 + neighbours)

    pending = []
    for t, (src, dst, recv) in enumerate(tensors):
        for k in range(1, group):
            to = (g + k) % group
            copy = pltpu.make_async_remote_copy(
                src_ref=strip(src, columns(to)),
                dst_ref=dst.at[z, g],
                send_sem=a2a_send.at[t, k],
                recv_sem=recv.at[z, g],
                device_id=(z * group + to, y),
                device_id_type=MESH,
            )
            copy.start()
            pending.append(copy)

    def hop(t, up, level, which, step, k, short):
        _, buf, recv = tensors[t]
        block = strip(buf.at[level, which], near) if short else buf.at[level, which]
        return pltpu.make_async_remote_copy(
            src_ref=block,
            dst_ref=block,
            send_sem=fwd_send.at[t, up, step, k],
            recv_sem=recv.at[level, which],
            device_id=(dom + group if up else dom - group, y),
            device_id_type=MESH,
        )

    def push(t, up, level, which, step, k, verb):
        exists, short = (has_up, up_end) if up else (has_down, down_end)

        @pl.when(both(exists, short))
        def _():
            getattr(hop(t, up, level, which, step, k, True), verb)()

        @pl.when(both(exists, jnp.logical_not(short)))
        def _():
            getattr(hop(t, up, level, which, step, k, False), verb)()

    def chain_step(t, step):
        for k in range(group):
            which = (g + group - k) % group
            if step == 0:
                if k == 0:
                    locals_[t].wait()
                else:
                    hop(t, 1, z, which, step, k, False).wait_recv()
                push(t, 1, z, which, step, k, "start")
                push(t, 0, z, which, step, k, "start")
                continue

            @pl.when(z >= step)
            def _():
                @pl.when(is_end)
                def _():
                    hop(t, 1, z - step, which, step, k, True).wait_recv()

                @pl.when(is_inner)
                def _():
                    hop(t, 1, z - step, which, step, k, False).wait_recv()

                push(t, 1, z - step, which, step, k, "start")

            @pl.when(z + step < layers)
            def _():
                @pl.when(is_end)
                def _():
                    hop(t, 0, z + step, which, step, k, True).wait_recv()

                @pl.when(is_inner)
                def _():
                    hop(t, 0, z + step, which, step, k, False).wait_recv()

                push(t, 0, z + step, which, step, k, "start")

    def chain_drain(t):
        for step in range(layers):
            for k in range(group):
                which = (g + group - k) % group

                @pl.when(z >= step)
                def _():
                    push(t, 1, z - step, which, step, k, "wait_send")

                @pl.when(z + step < layers)
                def _():
                    push(t, 0, z + step, which, step, k, "wait_send")

    def every(buf, field, far):
        if far:
            return buf[:, :, field, :, held:].reshape(count, spare)
        return buf[:, :, field, :, :held].reshape(count, held)

    def one(level, field, far):
        if far:
            return m_all[level, :, field, :, held:].reshape(slab, spare)
        return m_all[level, :, field, :, :held].reshape(slab, held)

    contract = (((1,), (1,)), ((), ()))

    def inner_product(left, right):
        return lax.dot_general(left, right, contract, preferred_element_type=jnp.float32)

    def block_of(buf, level, field, far):
        if far:
            return buf[level, :, field, :, held:].reshape(slab, spare)
        return buf[level, :, field, :, :held].reshape(slab, held)

    def rs_copy(level, to, slot, k, inner):
        span = pl.ds(0, 2 * piece + 8 if inner else piece)
        return pltpu.make_async_remote_copy(
            src_ref=part.at[level, to, span],
            dst_ref=inbox.at[level, slot, span],
            send_sem=rs_send.at[level, k],
            recv_sem=rs_recv.at[level, slot],
            device_id=layer_id(to),
            device_id_type=MESH,
        )

    def gram_level(level):
        own = jnp.zeros((slab, slab), jnp.float32)
        for field in range(fields):
            own += inner_product(one(z, field, False), block_of(m_all, level, field, False))
        part[level, :, :piece, :] = own.reshape(peers, piece, slab)

        @pl.when(is_inner)
        def _():
            mine = jnp.zeros((slab, slab), jnp.float32)
            other = jnp.zeros((slab, slab), jnp.float32)
            squares = jnp.zeros((8, slab), jnp.float32)
            for field in range(fields):
                far = block_of(m_all, level, field, True)
                mine += inner_product(one(z, field, True), far)
                other += inner_product(one(mate, field, True), far)
                for block in (block_of(m_all, level, field, False), far):
                    ones = jnp.ones((8, block.shape[1]), jnp.bfloat16)
                    wide = block.astype(jnp.float32)
                    wide = wide * wide
                    high = wide.astype(jnp.bfloat16)
                    low = (wide - high.astype(jnp.float32)).astype(jnp.bfloat16)
                    squares += inner_product(ones, high)
                    squares += inner_product(ones, low)
            part[level, :, :piece, :] += mine.reshape(peers, piece, slab)
            part[level, :, piece:2 * piece, :] = other.reshape(peers, piece, slab)
            part[level, :, 2 * piece:, :] = jnp.broadcast_to(squares[None], (peers, 8, slab))
            for k in range(1, peers):
                rs_copy(level, (me + k) % peers, me, k, True).start()
            inbox[level, me] = part[level, me]

        @pl.when(is_end)
        def _():
            for k in range(1, peers):
                rs_copy(level, (me + k) % peers, me, k, False).start()
            inbox[level, me, :piece] = part[level, me, :piece]

    def gram_step(step):
        @pl.when(z >= step)
        def _():
            gram_level(z - step)

        @pl.when(z + step < layers)
        def _():
            gram_level(z + step)

    chain_step(0, 0)

    @pl.when(is_end)
    def _():
        chain_step(1, 0)
        chain_step(2, 0)

    chain_step(0, 1)
    gram_level(z)
    gram_step(1)
    chain_step(0, 2)

    @pl.when(is_inner)
    def _():
        chain_step(1, 0)

    gram_step(2)
    chain_step(0, 3)
    gram_step(3)

    def swap(inner):
        span = pl.ds(0, piece + 8 if inner else piece)
        return pltpu.make_async_remote_copy(
            src_ref=swap_out.at[span],
            dst_ref=swap_in.at[span],
            send_sem=swap_sem.at[0],
            recv_sem=swap_sem.at[1],
            device_id=(mate * group + g, y),
            device_id_type=MESH,
        )

    def k_copy(half, to, slot, k):
        return pltpu.make_async_remote_copy(
            src_ref=krows.at[half, slot],
            dst_ref=krows.at[half, slot],
            send_sem=k_send.at[half, k],
            recv_sem=k_recv.at[half, slot],
            device_id=layer_id(to),
            device_id_type=MESH,
        )

    scale = scale_ref[0]

    def make_rows(half, level, row_gram, row_squares):
        first = level * slab + me * piece
        row_index = lax.broadcasted_iota(jnp.int32, (piece, count), 0) + first
        col_index = lax.broadcasted_iota(jnp.int32, (piece, count), 1)
        own_squares = jnp.sum(
            jnp.where(row_index == col_index, row_gram, 0.0), axis=1, keepdims=True
        )
        distance = own_squares + row_squares - 2.0 * row_gram
        divisor = jnp.full((piece, count), scale * total_cells, jnp.float32)
        krows[half, me] = jnp.exp(-distance / divisor).astype(jnp.bfloat16)
        for k in range(1, peers):
            k_copy(half, (me + k) % peers, me, k).start()

    def rs_finish(inner):
        span = slice(0, 2 * piece + 8 if inner else piece)
        totals = []
        for level in range(layers):
            for k in range(1, peers):
                source = (me + peers - k) % peers
                rs_copy(level, source, source, k, inner).wait_recv()
            total = inbox[level, 0, span]
            for k in range(1, peers):
                total = total + inbox[level, k, span]
            totals.append(total)
        return jnp.concatenate(totals, axis=1)

    @pl.when(is_end)
    def _():
        total = rs_finish(False)
        swap_out[:piece] = total
        swap(False).start()
        swap(True).wait_recv()
        make_rows(0, z, total + swap_in[:piece], swap_in[piece:piece + 1])

    @pl.when(is_inner)
    def _():
        chain_step(1, 1)
        chain_step(2, 0)
        total = rs_finish(True)
        swap_out[...] = total[piece:]
        swap(True).start()
        make_rows(0, z, total[:piece], total[2 * piece:2 * piece + 1])
        chain_step(1, 2)
        swap(False).wait_recv()
        make_rows(1, mate, total[piece:2 * piece] + swap_in[:piece], total[2 * piece:2 * piece + 1])
        chain_step(2, 1)

    def k_wait(half):
        for k in range(1, peers):
            source = (me + peers - k) % peers
            k_copy(half, source, source, k).wait_recv()

    def rowsum_of(kernel):
        return jnp.sum(kernel.astype(jnp.float32), axis=1, keepdims=True)

    def pulled_term(kernel, level, field, far):
        own = one(level, field, far).astype(jnp.float32)
        pulled = jnp.dot(kernel, every(m_all, field, far), preferred_element_type=jnp.float32)
        factor = 2.0 / jnp.full(own.shape, scale, jnp.float32)
        return factor * (rowsum_of(kernel) * own - pulled)

    def attract_term(kernel, field, far):
        buf = (g_zero, g_one)[field]
        block = buf[..., held:] if far else buf[..., :held]
        block = block.reshape(count, block.shape[-1])
        return jnp.dot(kernel, block, preferred_element_type=jnp.float32)

    k_wait(0)
    kernel = krows[0].reshape(slab, count)
    for field in range(fields):
        base[field, :, :held] = pulled_term(kernel, z, field, False)

    @pl.when(is_inner)
    def _():
        k_wait(1)
        mine = krows[0].reshape(slab, count)
        theirs = krows[1].reshape(slab, count)
        for field in range(fields):
            base[field, :, held:] = pulled_term(mine, z, field, True)
            base_far[field] = pulled_term(theirs, mate, field, True)

    def far_copy(field, to, source):
        return pltpu.make_async_remote_copy(
            src_ref=outbox_far.at[field, to],
            dst_ref=out_ref.at[field, :, columns(source, held, spare)],
            send_sem=o_send.at[1, field, to],
            recv_sem=o_recv.at[1, field, source],
            device_id=(mate * group + to, y),
            device_id_type=MESH,
        )

    def out_copy(field, to, source, inner):
        size = cells if inner else held
        return pltpu.make_async_remote_copy(
            src_ref=outbox.at[field, to, :, pl.ds(0, size)],
            dst_ref=out_ref.at[field, :, columns(source, 0, size)],
            send_sem=o_send.at[0, field, to],
            recv_sem=o_recv.at[0, field, source],
            device_id=(z * group + to, y),
            device_id_type=MESH,
        )

    for field in range(fields):
        @pl.when(is_end)
        def _():
            for step in range(1, layers):
                chain_step(1 + field, step)

        if field == 0:
            @pl.when(is_inner)
            def _():
                chain_step(2, 2)

        @pl.when(is_inner)
        def _():
            mine = krows[0].reshape(slab, count)
            theirs = krows[1].reshape(slab, count)
            update = (attract_term(theirs, field, True) + base_far[field]) * (1.0 / count)
            outbox_far[field] = update.reshape(group, rows, spare)
            for to in range(group):
                far_copy(field, to, g).start()
            update = (attract_term(mine, field, True) + base[field, :, held:]) * (1.0 / count)
            outbox[field, :, :, held:] = update.reshape(group, rows, spare)

        update = (attract_term(kernel, field, False) + base[field, :, :held]) * (1.0 / count)
        outbox[field, :, :, :held] = update.reshape(group, rows, held)

        @pl.when(is_inner)
        def _():
            for k in range(1, group):
                out_copy(field, (g + k) % group, g, True).start()
            out_ref[field, :, columns(g)] = outbox[field, g]

        @pl.when(is_end)
        def _():
            for k in range(1, group):
                out_copy(field, (g + k) % group, g, False).start()
            out_ref[field, :, columns(g, 0, held)] = outbox[field, g, :, :held]

    chain_drain(0)
    chain_drain(1)
    chain_drain(2)
    for copy in pending:
        copy.wait_send()

    @pl.when(is_inner)
    def _():
        for k in range(1, peers):
            for level in range(layers):
                rs_copy(level, (me + k) % peers, me, k, True).wait_send()
            k_copy(0, (me + k) % peers, me, k).wait_send()
            k_copy(1, (me + k) % peers, me, k).wait_send()
        swap(True).wait_send()
        for field in range(fields):
            for k in range(1, group):
                out_copy(field, (g + k) % group, g, True).wait_send()
                source = (g + group - k) % group
                out_copy(field, source, source, True).wait_recv()
            for to in range(group):
                far_copy(field, to, g).wait_send()

    @pl.when(is_end)
    def _():
        for k in range(1, peers):
            for level in range(layers):
                rs_copy(level, (me + k) % peers, me, k, False).wait_send()
            k_copy(0, (me + k) % peers, me, k).wait_send()
        swap(False).wait_send()
        for field in range(fields):
            for k in range(1, group):
                out_copy(field, (g + k) % group, g, False).wait_send()
                source = (g + group - k) % group
                out_copy(field, source, source, False).wait_recv()
            for source in range(group):
                far_copy(field, source, source).wait_recv()


def fused_body(layers, group, planes, models, gradients, length_scale):
    fields, rows, width = models.shape
    cells = width // group
    slab = group * rows
    count = layers * slab
    peers = group * planes
    piece = slab // peers
    held = cells // 2
    dma = pltpu.SemaphoreType.DMA
    return pl.pallas_call(
        functools.partial(stein_kernel, layers, group, planes, held),
        out_shape=jax.ShapeDtypeStruct(models.shape, jnp.float32),
        in_specs=[
            pl.BlockSpec(memory_space=pltpu.SMEM),
            pl.BlockSpec(memory_space=pl.ANY),
            pl.BlockSpec(memory_space=pl.ANY),
        ],
        out_specs=pl.BlockSpec(memory_space=pltpu.VMEM),
        scratch_shapes=[
            pltpu.VMEM((layers, group, fields, rows, cells), jnp.bfloat16),
            pltpu.VMEM((layers, group, rows, cells), jnp.bfloat16),
            pltpu.VMEM((layers, group, rows, cells), jnp.bfloat16),
            pltpu.VMEM((layers, peers, 2 * piece + 8, slab), jnp.float32),
            pltpu.VMEM((layers, peers, 2 * piece + 8, slab), jnp.float32),
            pltpu.VMEM((piece + 8, count), jnp.float32),
            pltpu.VMEM((piece + 8, count), jnp.float32),
            pltpu.VMEM((2, peers, piece, count), jnp.bfloat16),
            pltpu.VMEM((fields, slab, cells), jnp.float32),
            pltpu.VMEM((fields, slab, cells - held), jnp.float32),
            pltpu.VMEM((fields, group, rows, cells), jnp.float32),
            pltpu.VMEM((fields, group, rows, cells - held), jnp.float32),
            dma((3,)),
            dma((3, group)),
            dma((3, layers, group)),
            dma((3, 2, layers, group)),
            dma((layers, peers)),
            dma((layers, peers)),
            dma((2,)),
            dma((2, peers)),
            dma((2, peers)),
            dma((2, fields, group)),
            dma((2, fields, group)),
        ],
        compiler_params=pltpu.CompilerParams(collective_id=0, has_side_effects=True),
        name="stein",
    )(length_scale, models, gradients)


def solution(mesh):
    spread, planes = mesh.shape["dom"], mesh.shape["cell"]
    layers = math.isqrt(spread)
    group = spread // layers

    def body(models, gradients, length_scale):
        _, rows, width = models.shape
        fits = (
            layers == 4
            and models.shape[0] == 2
            and layers * group == spread
            and width % (group * 512) == 0
            and rows % 16 == 0
            and (group * rows) % 128 == 0
            and (group * rows) % (group * planes * 16) == 0
        )
        if not fits:
            return plain_body(models, gradients, length_scale)
        return fused_body(layers, group, planes, models, gradients, length_scale)

    placed = (P(None, "dom", "cell"), P(None, "dom", "cell"), P())
    return jax.shard_map(
        body, mesh=mesh, in_specs=placed, out_specs=P(None, "dom", "cell"), check_vma=False
    )
```
